256 devices in a mesh: out: 128 (over z, y, x), con: 2 (over core).
Axes of the slice: x: 4, y: 4, z: 8, core: 2. Of those that a mesh axis runs over, the one named last changes fastest.
Arguments:
- amplitudes: bfloat16 [512, 9216], P(('out', 'con')), may hold values from -6 to 6
- integrals: bfloat16 [131072, 9216], P('out', 'con'), may hold values from -0.078125 to 0.078125
- block_sizes: int32 [8], replicated, may hold values from 64 to 192, as said below
Outputs:
- ladder: bfloat16 [512, 131072], P('con', 'out')
The draws below stay inside these ranges and needn't reach their ends.
Inputs may be any that keep to these rules, and one draw needn't show every extreme that they name: `block_sizes`: each entry lies between 64 and 192; the entries sum to 1024; one entry equals 192 and one equals 64.
All inputs are finite; a program needn't handle non-finite values.
Results may differ from the reference program's by a relative error of at most 0.001.
Values may be sent and summed in bfloat16 or wider, within the bound.
A program may use at most 64 MiB of HBM per device.

```python
import jax
import jax.numpy as jnp
from jax import lax

NVIR = 1024
NIRREP = 8
DMAX = 192
CW = 6
OPAIRS = 512
ROWS_OUT = 1024
OUTP = 131072
NCOL = 9216
N_OUT = 128


def draw_block_sizes(key, part):
    first_key, second_key = jax.random.split(key)
    middle = NVIR // NIRREP
    lowest = 2 * middle - DMAX
    half_count = (NIRREP - 2) // 2
    deltas = jax.random.randint(first_key, (half_count,), lowest - middle, DMAX - middle + 1)
    values = jnp.concatenate([jnp.array([lowest, DMAX], dtype=jnp.int32), (middle + deltas).astype(jnp.int32), (middle - deltas).astype(jnp.int32)])
    order = jax.random.permutation(second_key, NIRREP)
    return values[order].astype(jnp.int32)


def levels(rng, shape, pieces, least, high):
    def one(dim, blocks):
        draws = jax.random.uniform(jax.random.fold_in(jax.random.fold_in(rng, 6), dim), (blocks,), jnp.float32, least / len(pieces), high / len(pieces))
        return jnp.repeat(jnp.exp(draws), shape[dim] // blocks).reshape((-1,) + (1,) * (len(shape) - dim - 1))

    level = one(*pieces[0])
    for cut in pieces[1:]:
        level = level * one(*cut)
    return level


def bell_draw(key, shape, spread, limit, pieces=(), kind=jnp.bfloat16):
    values = spread * jax.random.normal(key, shape, jnp.float32)
    if pieces:
        values = values * levels(key, shape, pieces, -0.22, 0.18)
    return jnp.clip(values, -limit, limit).astype(kind)


def setup_inputs(seed: int = 0) -> dict:
    arg_keys = jax.random.split(jax.random.key(seed), 4)
    amplitudes = bell_draw(arg_keys[0], (OPAIRS, NCOL), 1.0, 6.0, ((0, 256),))
    integrals = bell_draw(arg_keys[1], (OUTP, NCOL), (CW * NVIR) ** -0.5, 0.078125, ((0, 128), (1, 2)))
    block_sizes = draw_block_sizes(jax.random.fold_in(arg_keys[3], 71), 0)
    return {"amplitudes": amplitudes, "integrals": integrals, "block_sizes": block_sizes}


def reference(amplitudes, integrals, block_sizes):
    blocked = amplitudes.reshape(OPAIRS, NIRREP, CW, DMAX)
    valid_cols = jnp.arange(DMAX, dtype=jnp.int32)[None, :] < block_sizes[:, None]
    masked = jnp.where(valid_cols[None, :, None, :], blocked, jnp.zeros((), amplitudes.dtype))
    masked = masked.reshape(OPAIRS, NCOL).astype(jnp.float32)
    row_blocks = integrals.reshape(N_OUT, ROWS_OUT, NCOL)

    def one_block(row_block):
        return lax.dot_general(masked, row_block.astype(jnp.float32), (((1,), (1,)), ((), ())),
                               precision=lax.Precision.HIGHEST, preferred_element_type=jnp.float32)

    results = lax.map(one_block, row_blocks)
    ladder = jnp.transpose(results, (1, 0, 2)).reshape(OPAIRS, OUTP)
    return ladder.astype(jnp.bfloat16)
```

```python
import jax
import jax.numpy as jnp
from jax import lax
from jax.sharding import PartitionSpec as P

DMAX = 192


def mask_slots(amplitudes, block_sizes):
    row_count = amplitudes.shape[0]
    nirrep = block_sizes.shape[0]
    blocked = amplitudes.reshape(row_count, nirrep, -1, DMAX)
    valid_cols = jnp.arange(DMAX, dtype=jnp.int32)[None, :] < block_sizes[:, None]
    masked = jnp.where(valid_cols[None, :, None, :], blocked, jnp.zeros((), amplitudes.dtype))
    return masked.reshape(row_count, -1)


def contract(amp_rows, integrals):
    return lax.dot_general(
        amp_rows, integrals, (((1,), (1,)), ((), ())), preferred_element_type=jnp.float32
    )


def on_device(amplitudes, integrals, block_sizes):
    masked = mask_slots(amplitudes, block_sizes)
    con = lax.axis_index("con")
    con_count = lax.axis_size("con")
    half = integrals.shape[1]
    chip_rows = lax.all_gather(masked, "con", axis=0, tiled=True)
    own_cols = lax.dynamic_slice_in_dim(chip_rows, con * half, half, axis=1)
    all_rows = lax.all_gather(own_cols, "out", axis=0, tiled=True)
    out_rows = all_rows.shape[0] // con_count
    other = 1 - con
    other_part = contract(
        lax.dynamic_slice_in_dim(all_rows, other * out_rows, out_rows, axis=0), integrals
    )
    received = lax.ppermute(other_part, "con", perm=[(0, 1), (1, 0)])
    own_part = contract(
        lax.dynamic_slice_in_dim(all_rows, con * out_rows, out_rows, axis=0), integrals
    )
    own_part = lax.optimization_barrier(own_part)
    return (own_part + received).astype(jnp.bfloat16)


def solution(mesh):
    in_specs = (P(("out", "con"), None), P("out", "con"), P())
    out_specs = P("con", "out")
    return jax.shard_map(
        on_device, mesh=mesh, in_specs=in_specs, out_specs=out_specs, check_vma=False
    )
```

```python
import jax
import jax.numpy as jnp
from jax import lax
from jax.sharding import Mesh, PartitionSpec as P

DMAX = 192
TORUS = {128: (("z", 8), ("y", 4), ("x", 4))}


def mask_slots(amplitudes, block_sizes):
    row_count = amplitudes.shape[0]
    nirrep = block_sizes.shape[0]
    blocked = amplitudes.reshape(row_count, nirrep, -1, DMAX)
    valid_cols = jnp.arange(DMAX, dtype=jnp.int32)[None, :] < block_sizes[:, None]
    masked = jnp.where(valid_cols[None, :, None, :], blocked, jnp.zeros((), amplitudes.dtype))
    return masked.reshape(row_count, -1)


def contract(amp_rows, integrals):
    return lax.dot_general(
        amp_rows, integrals, (((1,), (1,)), ((), ())), preferred_element_type=jnp.float32
    )


def make_on_device(out_axes):
    def on_device(amplitudes, integrals, block_sizes):
        masked = mask_slots(amplitudes, block_sizes)
        con = lax.axis_index("con")
        con_count = lax.axis_size("con")
        half = integrals.shape[1]
        chip_rows = lax.all_gather(masked, "con", axis=0, tiled=True)
        all_rows = lax.dynamic_slice_in_dim(chip_rows, con * half, half, axis=1)
        for name in reversed(out_axes):
            all_rows = lax.all_gather(all_rows, name, axis=0, tiled=True)
        out_rows = all_rows.shape[0] // con_count
        other = 1 - con
        other_part = contract(
            lax.dynamic_slice_in_dim(all_rows, other * out_rows, out_rows, axis=0), integrals
        )
        received = lax.ppermute(other_part, "con", perm=[(0, 1), (1, 0)])
        own_part = contract(
            lax.dynamic_slice_in_dim(all_rows, con * out_rows, out_rows, axis=0), integrals
        )
        own_part = lax.optimization_barrier(own_part)
        return (own_part + received).astype(jnp.bfloat16)

    return on_device


def solution(mesh):
    n_out = mesh.shape["out"]
    axes = TORUS.get(n_out, (("out", n_out),))
    names = tuple(name for name, _ in axes)
    devices = mesh.devices.reshape(tuple(size for _, size in axes) + (mesh.shape["con"],))
    torus_mesh = Mesh(devices, names + ("con",))
    in_specs = (P(names + ("con",), None), P(names, "con"), P())
    out_specs = P("con", names)
    return jax.shard_map(
        make_on_device(names), mesh=torus_mesh, in_specs=in_specs, out_specs=out_specs,
        check_vma=False,
    )
```
